32 devices in a mesh: row: 4 (over z), col: 4 (over x, core), layer: 2 (over y).
Axes of the slice: x: 2, y: 2, z: 4, core: 2. Of those that a mesh axis runs over, the one named last changes fastest.
Arguments:
- left_blocks: float32 [4, 2, 4, 4, 128, 128], P('row', 'layer', 'col'), may hold values from -1.2 to 1.2
- right_blocks: float32 [2, 4, 4, 8, 128, 128], P('layer', 'row', 'col'), may hold values from -1.2 to 1.2
- pair_stacks: int32 [4, 4, 2, 4, 3, 32], P('row', 'col', 'layer'), may hold values from 0 to 32, as said below
Outputs:
- product_window: float32 [4, 4, 32, 128, 128], P('row', 'col', 'layer')
The draws below stay inside these ranges and needn't reach their ends.
Inputs may be any that keep to these rules, and one draw needn't show every extreme that they name: `pair_stacks`: entry 0 of a list holds left slots below 4, entry 1 right slots below 8, entry 2 product blocks below 32; the live triples stand first, every other slot holds (0, 0, 32); some list is live in all 32 slots.
All inputs are finite; a program needn't handle non-finite values.
Results may differ from the reference program's by a relative error of at most 0.0003.
Values sent between devices are 32-bit elements; how exact they have to be, the bound alone decides.
A program may use at most 64 MiB of HBM per device.

```python
import jax
import jax.numpy as jnp
from jax import lax

BS = 128
SA = 4
SB = 8
PCAP = 32
OUT_TILE = 32
ROW_TILES = 4
COL_TILES = 4
K_PARTS = 2
PIECES = 4


def draw_pair_stacks(key, part):
    grid_shape = (ROW_TILES, COL_TILES, K_PARTS, PIECES)
    key_tile, key_piece, key_chosen, key_left, key_right, key_out = jax.random.split(key, 6)
    tile_load = jax.random.randint(key_tile, (ROW_TILES, COL_TILES, 1, 1), 8, 33)
    piece_load = jax.random.randint(key_piece, grid_shape, 24, 33)
    live_counts = PCAP * tile_load * piece_load // 1024
    flat_loads = live_counts.reshape(-1)
    chosen = jax.random.randint(key_chosen, (), 0, flat_loads.shape[0])
    flat_loads = jnp.where(jnp.arange(flat_loads.shape[0]) == chosen, PCAP, flat_loads)
    live_counts = flat_loads.reshape(grid_shape)
    slot_ids = jnp.arange(PCAP)
    live_mask = slot_ids < live_counts[..., None]
    left_slot = jax.random.randint(key_left, grid_shape + (PCAP,), 0, SA)
    right_slot = jax.random.randint(key_right, grid_shape + (PCAP,), 0, SB)
    out_slot = jax.random.randint(key_out, grid_shape + (PCAP,), 0, OUT_TILE)
    left_slot = jnp.where(live_mask, left_slot, 0)
    right_slot = jnp.where(live_mask, right_slot, 0)
    out_slot = jnp.where(live_mask, out_slot, OUT_TILE)
    return jnp.stack([left_slot, right_slot, out_slot], axis=-2).astype(jnp.int32)


def level_of(own_key, shape, cuts, least, high):
    gain = 1.0
    for axis_at, shards_of in cuts:
        draws = jax.random.uniform(jax.random.fold_in(jax.random.fold_in(own_key, 6), axis_at), (shards_of,), jnp.float32, least / len(cuts), high / len(cuts))
        gain = gain * jnp.repeat(jnp.exp(draws), shape[axis_at] // shards_of).reshape((-1,) + (1,) * (len(shape) - 1 - axis_at))
    return gain


def bell_draw(own_key, dims, deviation, most, shards=(), held_as=jnp.bfloat16):
    entries = deviation * jax.random.normal(own_key, dims, jnp.float32)
    if shards:
        entries = entries * level_of(own_key, dims, shards, -0.22, 0.18)
    return jnp.clip(entries, -most, most).astype(held_as)


def setup_inputs(seed: int = 0) -> dict:
    arg_keys = jax.random.split(jax.random.key(seed), 4)
    return {
        "left_blocks": bell_draw(arg_keys[0], (ROW_TILES, K_PARTS, PIECES, SA, BS, BS), 0.15, 1.2, ((0, 4), (1, 2), (2, 4)), jnp.float32),
        "right_blocks": bell_draw(arg_keys[1], (K_PARTS, PIECES, COL_TILES, SB, BS, BS), 0.15, 1.2, ((0, 2), (1, 4), (2, 4)), jnp.float32),
        "pair_stacks": draw_pair_stacks(jax.random.fold_in(arg_keys[3], 71), 0),
    }


def reference(left_blocks, right_blocks, pair_stacks):
    layer_ids = jnp.arange(K_PARTS).astype(jnp.int32)[:, None, None]
    piece_ids = jnp.arange(PIECES).astype(jnp.int32)[None, :, None]

    def tile_sum(tile_index):
        row_index = tile_index // COL_TILES
        col_index = tile_index % COL_TILES
        stacks = pair_stacks[row_index, col_index]
        left_tile = left_blocks[row_index]
        right_tile = right_blocks[:, :, col_index]
        left_slot = stacks[:, :, 0, :]
        right_slot = stacks[:, :, 1, :]
        out_slot = stacks[:, :, 2, :]
        first_blocks = left_tile[layer_ids, piece_ids, left_slot]
        second_blocks = right_tile[layer_ids, piece_ids, right_slot]
        products = jnp.einsum("lpqxy,lpqyz->lpqxz", first_blocks, second_blocks,
                              precision=lax.Precision.HIGHEST)
        summed = jax.ops.segment_sum(products.reshape(-1, BS, BS), out_slot.reshape(-1),
                                     num_segments=OUT_TILE + 1)
        return summed[:OUT_TILE]

    tiles = lax.map(tile_sum, jnp.arange(ROW_TILES * COL_TILES).astype(jnp.int32))
    return tiles.reshape(ROW_TILES, COL_TILES, OUT_TILE, BS, BS)
```

```python
import functools

import jax
import jax.numpy as jnp
from jax import lax
from jax.experimental import pallas as pl
from jax.experimental.pallas import tpu as pltpu
from jax.sharding import PartitionSpec as P

OUT_TILE = 32
MESH = pl.DeviceIdType.MESH


def kernel(
    rows, cols, left_ref, right_ref, stacks_ref, out_ref,
    left_all, right_all, lists, tab_v, tab_s, pairs, wide, deep, low, buf,
    ring_send, ring_recv, ly_send, ly_recv, lc_send, lc_recv, st_send, st_recv, tab_sem,
):
    held, sa, bs, _ = left_ref.shape
    sb = right_ref.shape[0]
    half = sb // 2
    pieces, _, cap = stacks_ref.shape
    outs = out_ref.shape[0]
    ring = 2 * rows
    last_send = ring - 2

    row = lax.axis_index("row")
    col = lax.axis_index("col")
    layer = lax.axis_index("layer")
    other = 1 - layer

    def place(layer_at, row_at):
        return jnp.where(layer_at == 0, row_at, ring - 1 - row_at)

    def unplace(spot):
        return jnp.where(spot < rows, 0, 1), jnp.where(spot < rows, spot, ring - 1 - spot)

    def wrap(spot):
        return lax.rem(spot + 2 * ring, ring)

    me = place(layer, row)
    cw_layer, cw_row = unplace(wrap(me + 1))
    cc_layer, cc_row = unplace(wrap(me - 1))
    right_id = {"row": cw_row, "col": col, "layer": cw_layer}
    left_id = {"row": cc_row, "col": col, "layer": cc_layer}
    twin_id = {"row": row, "col": col, "layer": other}

    def peer_id(step):
        return {"row": row, "col": lax.rem(col + step, cols), "layer": layer}

    barrier = pltpu.get_barrier_semaphore()
    for target in (right_id, left_id, twin_id) + tuple(peer_id(j) for j in range(1, cols)):
        pl.semaphore_signal(barrier, inc=1, device_id=target, device_id_type=MESH)
    pl.semaphore_wait(barrier, 3 + cols - 1)

    def remote(src, dst, send, recv, target):
        return pltpu.make_async_remote_copy(
            src_ref=src, dst_ref=dst, send_sem=send, recv_sem=recv,
            device_id=target, device_id_type=MESH)

    def ring_copy(way, step, spot, part, own=False):
        slot = right_all.at[spot, pl.ds(part * half, half)]
        src = right_ref.at[pl.ds(part * half, half)] if own else slot
        return remote(src, slot, ring_send.at[way, step], ring_recv.at[way, step],
                      right_id if way == 0 else left_id)

    def send_ring(step, own=False):
        part = lax.rem(step, 2)
        ring_copy(0, step, wrap(me - step // 2), part, own).start()
        ring_copy(1, step, wrap(me + step // 2), 1 - part, own).start()

    def await_ring(step):
        part = lax.rem(step, 2)
        ring_copy(0, step, wrap(me - 1 - step // 2), part).wait_recv()
        ring_copy(1, step, wrap(me + 1 + step // 2), 1 - part).wait_recv()

    stack_copy = remote(stacks_ref, lists.at[layer], st_send, st_recv, twin_id)
    stack_copy.start()

    def twin_copy(i):
        return remote(left_ref.at[i], left_all.at[layer, col * held + i],
                      ly_send.at[i], ly_recv.at[i], twin_id)

    def twin_arrival(i):
        return remote(left_ref.at[i], left_all.at[other, col * held + i],
                      ly_send.at[i], ly_recv.at[i], twin_id)

    def peer_copy(kind, i, j):
        at = (layer if kind == 0 else other), col * held + i
        src = left_ref.at[i] if kind == 0 else left_all.at[at]
        return remote(src, left_all.at[at], lc_send.at[kind, i, j - 1], lc_recv.at[kind, i, j - 1], peer_id(j))

    def peer_arrival(kind, i, j):
        at = (layer if kind == 0 else other), lax.rem(col - j + cols, cols) * held + i
        return remote(left_all.at[at], left_all.at[at], lc_send.at[kind, i, j - 1],
                      lc_recv.at[kind, i, j - 1], peer_id(j))

    for i in range(held):
        twin_copy(i).start()
    send_ring(0, True)
    for i in range(held):
        for j in range(1, cols):
            peer_copy(0, i, j).start()
    send_ring(1, True)

    lists[layer] = stacks_ref[...]
    for i in range(held):
        left_all[layer, col * held + i] = left_ref[i]
    right_all[me] = right_ref[...]
    for o in range(outs + 1):
        buf[cap + o] = jnp.zeros((bs, bs), jnp.float32)

    remote(stacks_ref, lists.at[other], st_send, st_recv, twin_id).wait_recv()

    def gathered(entry):
        return jnp.concatenate(
            [lists[t // pieces, t % pieces, entry:entry + 1, :] for t in range(2 * pieces)], axis=0)

    out_at = gathered(2) - layer * outs
    out_at = jnp.where((out_at >= 0) & (out_at < outs), out_at, outs)
    lane = lax.broadcasted_iota(jnp.int32, out_at.shape, 1)
    before = cap + out_at
    final = cap + jnp.minimum(lane, outs)
    for q in range(cap):
        mine = out_at[:, q:q + 1]
        before = jnp.where((out_at == mine) & (lane > q), q, before)
        final = jnp.where(lane == mine, q, final)
    tab_v[0, :, :cap] = gathered(1) * sa + gathered(0)
    tab_v[1, :, :cap] = before
    tab_v[2, :, :cap] = final
    tab_copy = pltpu.make_async_copy(tab_v, tab_s, tab_sem)
    tab_copy.start()

    for i in range(held):
        twin_arrival(i).wait_recv()
        for j in range(1, cols):
            peer_copy(1, i, j).start()
    tab_copy.wait()

    def split(value):
        high = value.astype(jnp.bfloat16)
        return high, (value - high.astype(jnp.float32)).astype(jnp.bfloat16)

    def accumulate(spot, last=False):
        layer_at, row_at = unplace(spot)
        at = layer_at * pieces + row_at
        for a in range(sa):
            high, rest = split(left_all[layer_at, row_at, a])
            wide[a * bs:(a + 1) * bs, :bs] = high
            wide[a * bs:(a + 1) * bs, bs:] = rest
        for b in range(0, sb, 2):
            for n in range(2):
                high, rest = split(right_all[spot, b + n])
                for m in range(2):
                    deep[m * bs:(m + 1) * bs, n * bs:(n + 1) * bs] = high
                    low[m * bs:(m + 1) * bs, n * bs:(n + 1) * bs] = rest
            product = jnp.dot(wide[...], deep[...], preferred_element_type=jnp.float32)
            product += jnp.dot(wide[...], low[...], preferred_element_type=jnp.float32)
            for n in range(2):
                for a in range(sa):
                    pairs[(b + n) * sa + a] = product[a * bs:(a + 1) * bs, n * bs:(n + 1) * bs]

        def chain(q, carry):
            buf[q] = pairs[tab_s[0, at, q]] + buf[tab_s[1, at, q]]
            return carry

        lax.fori_loop(0, cap, chain, 0)

        def keep(o, carry):
            if last:
                out_ref[o] = buf[tab_s[2, at, o]]
            else:
                buf[cap + o] = buf[tab_s[2, at, o]]
            return carry

        lax.fori_loop(0, outs, keep, 0)

    def advance(d):
        await_ring(2 * d - 2)
        send_ring(2 * d)
        await_ring(2 * d - 1)

        @pl.when(2 * d + 1 <= last_send)
        def _():
            send_ring(2 * d + 1)

    advance(1)
    for kind in range(2):
        for i in range(held):
            for j in range(1, cols):
                peer_arrival(kind, i, j).wait_recv()

    def first(j, carry):
        accumulate(wrap(me + j - 1))
        return carry

    lax.fori_loop(0, 3, first, 0)

    def step(d, carry):
        advance(d)

        def side(j, inner):
            accumulate(wrap(me + (2 * j - 1) * d))
            return inner

        lax.fori_loop(0, 2, side, 0)
        return carry

    lax.fori_loop(2, rows, step, 0)
    await_ring(last_send)
    accumulate(wrap(me + rows), True)

    stack_copy.wait_send()
    for i in range(held):
        twin_copy(i).wait_send()
        for kind in range(2):
            for j in range(1, cols):
                peer_copy(kind, i, j).wait_send()

    def drain(s, carry):
        part = lax.rem(s, 2)
        ring_copy(0, s, wrap(me - s // 2), part).wait_send()
        ring_copy(1, s, wrap(me + s // 2), 1 - part).wait_send()
        return carry

    lax.fori_loop(0, last_send + 1, drain, 0)


def body(rows, cols, left_blocks, right_blocks, pair_stacks):
    left_local = left_blocks[0, 0]
    right_local = right_blocks[0, 0, 0]
    stacks = pair_stacks[0, 0, 0]
    held, sa, bs, _ = left_local.shape
    sb = right_local.shape[0]
    pieces, _, cap = stacks.shape
    outs = OUT_TILE // 2
    f32 = jnp.float32
    dma = pltpu.SemaphoreType.DMA
    vmem = pl.BlockSpec(memory_space=pltpu.VMEM)
    block = bs * bs * 4
    blocks = 2 * pieces * (sa + sb) + sa * sb + cap + 2 * outs + sb + held * sa + 16
    result = pl.pallas_call(
        functools.partial(kernel, rows, cols),
        out_shape=jax.ShapeDtypeStruct((outs, bs, bs), f32),
        in_specs=[vmem] * 3,
        out_specs=vmem,
        scratch_shapes=[
            pltpu.VMEM((2, pieces, sa, bs, bs), f32),
            pltpu.VMEM((2 * rows, sb, bs, bs), f32),
            pltpu.VMEM((2, pieces, 3, cap), jnp.int32),
            pltpu.VMEM((3, 2 * pieces, 128), jnp.int32),
            pltpu.SMEM((3, 2 * pieces, 128), jnp.int32),
            pltpu.VMEM((sa * sb, bs, bs), f32),
            pltpu.VMEM((sa * bs, 2 * bs), jnp.bfloat16),
            pltpu.VMEM((2 * bs, 2 * bs), jnp.bfloat16),
            pltpu.VMEM((2 * bs, 2 * bs), jnp.bfloat16),
            pltpu.VMEM((cap + outs + 1, bs, bs), f32),
            dma((2, 2 * rows - 1)),
            dma((2, 2 * rows - 1)),
            dma((held,)),
            dma((held,)),
            dma((2, held, cols - 1)),
            dma((2, held, cols - 1)),
            dma, dma, dma,
        ],
        compiler_params=pltpu.CompilerParams(
            collective_id=0, has_side_effects=True, vmem_limit_bytes=blocks * block + (6 << 20)),
        name="ring_window",
    )(left_local, right_local, stacks)
    return result[None, None]


def solution(mesh):
    placed = (
        P("row", "layer", "col", None, None, None),
        P("layer", "row", "col", None, None, None),
        P("row", "col", "layer", None, None, None),
    )
    return jax.shard_map(
        functools.partial(body, mesh.shape["row"], mesh.shape["col"]),
        mesh=mesh,
        in_specs=placed,
        out_specs=P("row", "col", "layer", None, None),
        check_vma=False,
    )
```

```python
import functools

import jax
import jax.numpy as jnp
from jax import lax
from jax.experimental import pallas as pl
from jax.experimental.pallas import tpu as pltpu
from jax.sharding import PartitionSpec as P

OUT_TILE = 32
MESH = pl.DeviceIdType.MESH


def kernel(
    rows, cols, left_ref, right_ref, stacks_ref, out_ref,
    left_all, right_all, lists, tab_v, tab_s, pairs, wide, deep, low, buf,
    ring_send, ring_recv, end_send, end_recv, ly_send, ly_recv, lc_send, lc_recv,
    st_send, st_recv, tab_sem, own_sem,
):
    held, sa, bs, _ = left_ref.shape
    sb = right_ref.shape[0]
    half = sb // 2
    _, pieces, cap = stacks_ref.shape
    outs = out_ref.shape[0]
    ring = 2 * rows
    quarter = sb // 4

    row = lax.axis_index("row")
    col = lax.axis_index("col")
    layer = lax.axis_index("layer")
    other = 1 - layer

    def place(layer_at, row_at):
        return jnp.where(layer_at == 0, row_at, ring - 1 - row_at)

    def unplace(spot):
        return jnp.where(spot < rows, 0, 1), jnp.where(spot < rows, spot, ring - 1 - spot)

    def wrap(spot):
        return lax.rem(spot + 2 * ring, ring)

    me = place(layer, row)
    cw_layer, cw_row = unplace(wrap(me + 1))
    cc_layer, cc_row = unplace(wrap(me - 1))
    right_id = {"row": cw_row, "col": col, "layer": cw_layer}
    left_id = {"row": cc_row, "col": col, "layer": cc_layer}
    twin_id = {"row": row, "col": col, "layer": other}

    def peer_id(step):
        return {"row": row, "col": lax.rem(col + step, cols), "layer": layer}

    barrier = pltpu.get_barrier_semaphore()
    for target in (right_id, left_id, twin_id) + tuple(peer_id(j) for j in range(1, cols)):
        pl.semaphore_signal(barrier, inc=1, device_id=target, device_id_type=MESH)

    own_copies = [
        pltpu.make_async_copy(right_ref, right_all.at[me], own_sem.at[0]),
        pltpu.make_async_copy(left_ref, left_all.at[layer, pl.ds(col * held, held)], own_sem.at[1]),
        pltpu.make_async_copy(stacks_ref, lists.at[layer], own_sem.at[2]),
    ]
    for copy in own_copies:
        copy.start()
    pl.semaphore_wait(barrier, 3 + cols - 1)

    def remote(src, dst, send, recv, target):
        return pltpu.make_async_remote_copy(
            src_ref=src, dst_ref=dst, send_sem=send, recv_sem=recv,
            device_id=target, device_id_type=MESH)

    def ring_copy(way, step, spot, part, own=False):
        slot = right_all.at[spot, pl.ds(part * half, half)]
        src = right_ref.at[pl.ds(part * half, half)] if own else slot
        return remote(src, slot, ring_send.at[way, step], ring_recv.at[way, step],
                      right_id if way == 0 else left_id)

    def send_ring(step, own=False):
        part = lax.rem(step, 2)
        ring_copy(0, step, wrap(me - step // 2), part, own).start()
        ring_copy(1, step, wrap(me + step // 2), 1 - part, own).start()

    def await_ring(step):
        part = lax.rem(step, 2)
        ring_copy(0, step, wrap(me - 1 - step // 2), part).wait_recv()
        ring_copy(1, step, wrap(me + 1 + step // 2), 1 - part).wait_recv()

    def by_cw(spot):
        by_layer = (spot == 0) | (spot == rows)
        by_row = (spot == rows - 1) | (spot == ring - 1)
        return jnp.where(by_layer, 1, jnp.where(by_row, 3, 2))

    def end_copy(way, t):
        spot = wrap(me - (rows - 1)) if way == 0 else wrap(me + rows - 1)
        slot = right_all.at[spot, pl.ds(t * quarter, quarter)]
        return remote(slot, slot, end_send.at[way, t], end_recv.at[t], right_id if way == 0 else left_id)

    cw_count, cc_count = by_cw(wrap(me + 1)), by_cw(wrap(me - 1))

    def ends(way, t, action):
        @pl.when(t < cw_count if way == 0 else t >= cc_count)
        def _():
            copy = end_copy(way, t)
            copy.start() if action == "start" else copy.wait_send()

    def await_end(t):
        slot = right_all.at[wrap(me + rows), pl.ds(t * quarter, quarter)]
        remote(slot, slot, end_send.at[0, t], end_recv.at[t], right_id).wait_recv()

    stack_copy = remote(stacks_ref, lists.at[layer], st_send, st_recv, twin_id)
    stack_copy.start()

    def twin_copy(i):
        return remote(left_ref.at[i], left_all.at[layer, col * held + i],
                      ly_send.at[i], ly_recv.at[i], twin_id)

    def twin_arrival(i):
        return remote(left_ref.at[i], left_all.at[other, col * held + i],
                      ly_send.at[i], ly_recv.at[i], twin_id)

    def peer_copy(kind, i, j):
        at = (layer if kind == 0 else other), col * held + i
        src = left_ref.at[i] if kind == 0 else left_all.at[at]
        return remote(src, left_all.at[at], lc_send.at[kind, i, j - 1], lc_recv.at[kind, i, j - 1], peer_id(j))

    def peer_arrival(kind, i, j):
        at = (layer if kind == 0 else other), lax.rem(col - j + cols, cols) * held + i
        return remote(left_all.at[at], left_all.at[at], lc_send.at[kind, i, j - 1],
                      lc_recv.at[kind, i, j - 1], peer_id(j))

    for i in range(held):
        twin_copy(i).start()
    send_ring(0, True)
    for i in range(held):
        for j in range(1, cols):
            peer_copy(0, i, j).start()
    send_ring(1, True)

    for o in range(outs + 1):
        buf[cap + o] = jnp.zeros((bs, bs), jnp.float32)

    for copy in own_copies:
        copy.wait()
    remote(stacks_ref, lists.at[other], st_send, st_recv, twin_id).wait_recv()

    def gathered(entry):
        return jnp.concatenate([lists[0, entry], lists[1, entry]], axis=0)

    out_at = gathered(2) - layer * outs
    out_at = jnp.where((out_at >= 0) & (out_at < outs), out_at, outs)
    lane = lax.broadcasted_iota(jnp.int32, out_at.shape, 1)
    before = cap + out_at
    final = cap + jnp.minimum(lane, outs)
    for q in range(cap):
        mine = out_at[:, q:q + 1]
        before = jnp.where((out_at == mine) & (lane > q), q, before)
        final = jnp.where(lane == mine, q, final)
    tab_v[0, :, :cap] = gathered(1) * sa + gathered(0)
    tab_v[1, :, :cap] = before
    tab_v[2, :, :cap] = final
    tab_copy = pltpu.make_async_copy(tab_v, tab_s, tab_sem)
    tab_copy.start()

    for i in range(held):
        twin_arrival(i).wait_recv()
        for j in range(1, cols):
            peer_copy(1, i, j).start()
    tab_copy.wait()

    def split(value):
        high = value.astype(jnp.bfloat16)
        return high, (value - high.astype(jnp.float32)).astype(jnp.bfloat16)

    def widen(spot):
        layer_at, row_at = unplace(spot)
        for a in range(sa):
            high, rest = split(left_all[layer_at, row_at, a])
            wide[a * bs:(a + 1) * bs, :bs] = high
            wide[a * bs:(a + 1) * bs, bs:] = rest

    def multiply(spot, b):
        for n in range(2):
            high, rest = split(right_all[spot, b + n])
            for m in range(2):
                deep[m * bs:(m + 1) * bs, n * bs:(n + 1) * bs] = high
                low[m * bs:(m + 1) * bs, n * bs:(n + 1) * bs] = rest
        product = jnp.dot(wide[...], deep[...], preferred_element_type=jnp.float32)
        product += jnp.dot(wide[...], low[...], preferred_element_type=jnp.float32)
        for n in range(2):
            for a in range(sa):
                pairs[(b + n) * sa + a] = product[a * bs:(a + 1) * bs, n * bs:(n + 1) * bs]

    def gather_sums(spot, target, offset):
        layer_at, row_at = unplace(spot)
        at = layer_at * pieces + row_at

        def chain(q, carry):
            buf[q] = pairs[tab_s[0, at, q]] + buf[tab_s[1, at, q]]
            return carry

        lax.fori_loop(0, cap, chain, 0, unroll=4)

        def keep(o, carry):
            target[offset + o] = buf[tab_s[2, at, o]]
            return carry

        lax.fori_loop(0, outs, keep, 0, unroll=4)

    def accumulate(spot):
        widen(spot)
        for b in range(0, sb, 2):
            multiply(spot, b)
        gather_sums(spot, buf, cap)

    def advance(d):
        await_ring(2 * d - 2)

        @pl.when(d < rows - 1)
        def _():
            send_ring(2 * d)

        @pl.when(d == rows - 1)
        def _():
            for t in range(2):
                ends(0, t, "start")
                ends(1, 3 - t, "start")

        await_ring(2 * d - 1)

        @pl.when(d < rows - 1)
        def _():
            send_ring(2 * d + 1)

        @pl.when(d == rows - 1)
        def _():
            ends(0, 2, "start")
            ends(1, 1, "start")

    advance(1)
    for kind in range(2):
        for i in range(held):
            for j in range(1, cols):
                peer_arrival(kind, i, j).wait_recv()

    def first(j, carry):
        accumulate(wrap(me + j - 1))
        return carry

    lax.fori_loop(0, 3, first, 0)

    def step(d, carry):
        advance(d)

        def side(j, inner):
            accumulate(wrap(me + (2 * j - 1) * d))
            return inner

        lax.fori_loop(0, 2, side, 0)
        return carry

    lax.fori_loop(2, rows, step, 0)
    opposite = wrap(me + rows)
    widen(opposite)
    stack_copy.wait_send()
    for i in range(held):
        twin_copy(i).wait_send()
        for kind in range(2):
            for j in range(1, cols):
                peer_copy(kind, i, j).wait_send()

    def drain(s, carry):
        part = lax.rem(s, 2)
        ring_copy(0, s, wrap(me - s // 2), part).wait_send()
        ring_copy(1, s, wrap(me + s // 2), 1 - part).wait_send()
        return carry

    lax.fori_loop(0, ring - 2, drain, 0)
    for t in (0, 3, 1, 2):
        await_end(t)
        for b in range(t * quarter, (t + 1) * quarter, 2):
            multiply(opposite, b)
    gather_sums(opposite, out_ref, 0)
    for t in range(3):
        ends(0, t, "wait")
        ends(1, 3 - t, "wait")


def body(rows, cols, left_blocks, right_blocks, pair_stacks):
    left_local = left_blocks[0, 0]
    right_local = right_blocks[0, 0, 0]
    stacks = jnp.swapaxes(pair_stacks[0, 0, 0], 0, 1)
    held, sa, bs, _ = left_local.shape
    sb = right_local.shape[0]
    _, pieces, cap = stacks.shape
    outs = OUT_TILE // 2
    f32 = jnp.float32
    dma = pltpu.SemaphoreType.DMA
    vmem = pl.BlockSpec(memory_space=pltpu.VMEM)
    block = bs * bs * 4
    blocks = 2 * pieces * (sa + sb) + sa * sb + cap + 2 * outs + sb + held * sa + 16
    result = pl.pallas_call(
        functools.partial(kernel, rows, cols),
        out_shape=jax.ShapeDtypeStruct((outs, bs, bs), f32),
        in_specs=[pl.BlockSpec(memory_space=pltpu.HBM)] * 3,
        out_specs=vmem,
        scratch_shapes=[
            pltpu.VMEM((2, pieces, sa, bs, bs), f32),
            pltpu.VMEM((2 * rows, sb, bs, bs), f32),
            pltpu.VMEM((2, 3, pieces, cap), jnp.int32),
            pltpu.VMEM((3, 2 * pieces, 128), jnp.int32),
            pltpu.SMEM((3, 2 * pieces, 128), jnp.int32),
            pltpu.VMEM((sa * sb, bs, bs), f32),
            pltpu.VMEM((sa * bs, 2 * bs), jnp.bfloat16),
            pltpu.VMEM((2 * bs, 2 * bs), jnp.bfloat16),
            pltpu.VMEM((2 * bs, 2 * bs), jnp.bfloat16),
            pltpu.VMEM((cap + outs + 1, bs, bs), f32),
            dma((2, 2 * rows - 2)),
            dma((2, 2 * rows - 2)),
            dma((2, 4)),
            dma((4,)),
            dma((held,)),
            dma((held,)),
            dma((2, held, cols - 1)),
            dma((2, held, cols - 1)),
            dma, dma, dma,
            dma((3,)),
        ],
        compiler_params=pltpu.CompilerParams(
            collective_id=0, has_side_effects=True, vmem_limit_bytes=blocks * block + (6 << 20)),
        name="ring_window",
    )(left_local, right_local, stacks)
    return result[None, None]


def solution(mesh):
    placed = (
        P("row", "layer", "col", None, None, None),
        P("layer", "row", "col", None, None, None),
        P("row", "col", "layer", None, None, None),
    )
    return jax.shard_map(
        functools.partial(body, mesh.shape["row"], mesh.shape["col"]),
        mesh=mesh,
        in_specs=placed,
        out_specs=P("row", "col", "layer", None, None),
        check_vma=False,
    )
```

```python
import functools

import jax
import jax.numpy as jnp
from jax import lax
from jax.experimental import pallas as pl
from jax.experimental.pallas import tpu as pltpu
from jax.sharding import PartitionSpec as P

OUT_TILE = 32
MESH = pl.DeviceIdType.MESH


def kernel(
    rows, cols, left_ref, right_ref, stacks_ref, out_ref,
    left_all, right_all, lists, tab_v, tab_s, pairs, wide, buf,
    ring_send, ring_recv, end_send, end_recv, ly_send, ly_recv, lc_send, lc_recv,
    st_send, st_recv, tab_sem, own_sem,
):
    held, sa, bs, _ = left_ref.shape
    sb = right_ref.shape[0]
    half = sb // 2
    _, pieces, cap = stacks_ref.shape
    outs = out_ref.shape[0]
    ring = 2 * rows
    quarter = sb // 4

    row = lax.axis_index("row")
    col = lax.axis_index("col")
    layer = lax.axis_index("layer")
    other = 1 - layer

    def place(layer_at, row_at):
        return jnp.where(layer_at == 0, row_at, ring - 1 - row_at)

    def unplace(spot):
        return jnp.where(spot < rows, 0, 1), jnp.where(spot < rows, spot, ring - 1 - spot)

    def wrap(spot):
        return lax.rem(spot + 2 * ring, ring)

    me = place(layer, row)
    cw_layer, cw_row = unplace(wrap(me + 1))
    cc_layer, cc_row = unplace(wrap(me - 1))
    right_id = {"row": cw_row, "col": col, "layer": cw_layer}
    left_id = {"row": cc_row, "col": col, "layer": cc_layer}
    twin_id = {"row": row, "col": col, "layer": other}

    chips = cols // 2
    sibling = col + 1 - 2 * lax.rem(col, 2)
    sibling_id = {"row": row, "col": sibling, "layer": layer}

    def peer_col(step):
        return lax.rem(col + 2 * step, cols)

    def peer_id(step):
        return {"row": row, "col": peer_col(step), "layer": layer}

    barrier = pltpu.get_barrier_semaphore()
    for target in (right_id, left_id, twin_id, sibling_id) + tuple(peer_id(j) for j in range(1, chips)):
        pl.semaphore_signal(barrier, inc=1, device_id=target, device_id_type=MESH)

    own_copies = [
        pltpu.make_async_copy(right_ref, right_all.at[me], own_sem.at[0]),
        pltpu.make_async_copy(left_ref, left_all.at[layer, pl.ds(col * held, held)], own_sem.at[1]),
        pltpu.make_async_copy(stacks_ref, lists.at[layer], own_sem.at[2]),
    ]
    for copy in own_copies:
        copy.start()
    pl.semaphore_wait(barrier, 3 + chips)

    def remote(src, dst, send, recv, target):
        return pltpu.make_async_remote_copy(
            src_ref=src, dst_ref=dst, send_sem=send, recv_sem=recv,
            device_id=target, device_id_type=MESH)

    def pick(way, ahead, back):
        return jnp.where(way == 0, ahead, back)

    def toward(way):
        return {"row": pick(way, cw_row, cc_row), "col": col, "layer": pick(way, cw_layer, cc_layer)}

    def ring_copy(way, step, away, own=False):
        spot = wrap(me - (1 - 2 * way) * away)
        part = pick(way, lax.rem(step, 2), 1 - lax.rem(step, 2))
        slot = right_all.at[spot, pl.ds(part * half, half)]
        src = right_ref.at[pl.ds(part * half, half)] if own else slot
        return remote(src, slot, ring_send.at[way, step], ring_recv.at[way, step], toward(way))

    first_way = jnp.where((me == 0) | (me == rows), 1, 0)
    ways = (first_way, 1 - first_way)

    def send_ring(way, step, own=False):
        ring_copy(way, step, step // 2, own).start()

    def await_ring(way, step):
        ring_copy(way, step, 1 + step // 2).wait_recv()

    def by_cw(spot):
        by_layer = (spot == 0) | (spot == rows)
        by_row = (spot == rows - 1) | (spot == ring - 1)
        return jnp.where(by_layer, 1, jnp.where(by_row, 3, 2))

    cw_count, cc_count = by_cw(wrap(me + 1)), 4 - by_cw(wrap(me - 1))

    def end_copy(way, u):
        t = pick(way, u, 3 - u)
        slot = right_all.at[wrap(me - (1 - 2 * way) * (rows - 1)), pl.ds(t * quarter, quarter)]
        return remote(slot, slot, end_send.at[way, t], end_recv.at[t], toward(way))

    def send_end(way, u):
        @pl.when(u < pick(way, cw_count, cc_count))
        def _():
            end_copy(way, u).start()

    def drain_end(way, u):
        @pl.when(u < pick(way, cw_count, cc_count))
        def _():
            end_copy(way, u).wait_send()

    def await_end(t):
        slot = right_all.at[wrap(me + rows), pl.ds(t * quarter, quarter)]
        remote(slot, slot, end_send.at[0, t], end_recv.at[t], right_id).wait_recv()

    stack_copy = remote(stacks_ref, lists.at[layer], st_send, st_recv, twin_id)
    stack_copy.start()

    def twin_copy(i):
        return remote(left_ref.at[i], left_all.at[layer, col * held + i],
                      ly_send.at[i], ly_recv.at[i], twin_id)

    def twin_arrival(i):
        return remote(left_ref.at[i], left_all.at[other, col * held + i],
                      ly_send.at[i], ly_recv.at[i], twin_id)

    def left_copy(kind, i, slot):
        source, target = col, sibling_id
        if slot >= chips:
            source = peer_col(cols - slot + chips - 1)
        elif slot:
            target = peer_id(slot)
        at = (layer if kind == 0 else other), source * held + i
        src = left_ref.at[i] if kind == 0 and slot < chips else left_all.at[at]
        return remote(src, left_all.at[at], lc_send.at[kind, i, slot], lc_recv.at[kind, i, slot], target)

    def left_arrival(kind, i, slot):
        source = sibling
        if slot >= chips:
            source = lax.rem(sibling + 2 * (cols - slot + chips - 1), cols)
        elif slot:
            source = peer_col(cols - slot)
        at = (layer if kind == 0 else other), source * held + i
        return remote(left_all.at[at], left_all.at[at], lc_send.at[kind, i, slot],
                      lc_recv.at[kind, i, slot], sibling_id)

    def relay(kind):
        for i in range(held):
            for j in range(1, chips):
                left_arrival(kind, i, j).wait_recv()
                left_copy(kind, i, chips - 1 + j).start()

    for i in range(held):
        twin_copy(i).start()
    for way in ways:
        send_ring(way, 0, True)
    for i in range(held):
        for slot in range(chips - 1, -1, -1):
            left_copy(0, i, slot).start()
    for way in ways:
        send_ring(way, 1, True)

    for o in range(outs + 1):
        buf[cap + o] = jnp.zeros((bs, bs), jnp.float32)

    for copy in own_copies:
        copy.wait()
    remote(stacks_ref, lists.at[other], st_send, st_recv, twin_id).wait_recv()

    def gathered(entry):
        return jnp.concatenate([lists[0, entry], lists[1, entry]], axis=0)

    out_at = gathered(2) - layer * outs
    out_at = jnp.where((out_at >= 0) & (out_at < outs), out_at, outs)
    lane = lax.broadcasted_iota(jnp.int32, out_at.shape, 1)
    before = cap + out_at
    final = cap + jnp.minimum(lane, outs)
    for q in range(cap):
        mine = out_at[:, q:q + 1]
        before = jnp.where((out_at == mine) & (lane > q), q, before)
        final = jnp.where(lane == mine, q, final)
    tab_v[0, :, :cap] = gathered(1) * sa + gathered(0)
    tab_v[1, :, :cap] = before
    tab_v[2, :, :cap] = final
    tab_copy = pltpu.make_async_copy(tab_v, tab_s, tab_sem)
    tab_copy.start()

    for i in range(held):
        twin_arrival(i).wait_recv()
        for slot in range(chips - 1, -1, -1):
            left_copy(1, i, slot).start()
    tab_copy.wait()
    relay(0)

    def split(value):
        high = value.astype(jnp.bfloat16)
        return high, (value - high.astype(jnp.float32)).astype(jnp.bfloat16)

    def widen(spot):
        layer_at, row_at = unplace(spot)
        for a in range(sa):
            high, rest = split(left_all[layer_at, row_at, a])
            for n in range(4):
                wide[a * bs:(a + 1) * bs, n * bs:(n + 1) * bs] = rest if n % 2 else high

    def multiply(spot, b):
        parts = [split(right_all[spot, b + n]) for n in range(2)]
        deep = jnp.concatenate([parts[0][0], parts[1][0]], axis=1)
        low = jnp.concatenate([parts[0][1], parts[1][1]], axis=1)
        stacked = jnp.concatenate([deep, deep, low, low], axis=0)
        product = jnp.dot(wide[...], stacked, preferred_element_type=jnp.float32)
        for n in range(2):
            for a in range(sa):
                pairs[(b + n) * sa + a] = product[a * bs:(a + 1) * bs, n * bs:(n + 1) * bs]

    def gather_sums(spot, target, offset):
        layer_at, row_at = unplace(spot)
        at = layer_at * pieces + row_at

        def chain(q, carry):
            buf[q] = pairs[tab_s[0, at, q]] + buf[tab_s[1, at, q]]
            return carry

        lax.fori_loop(0, cap, chain, 0, unroll=8)

        def keep(o, carry):
            target[offset + o] = buf[tab_s[2, at, o]]
            return carry

        lax.fori_loop(0, outs, keep, 0, unroll=8)

    def accumulate(spot):
        widen(spot)
        for b in range(0, sb, 2):
            multiply(spot, b)
        gather_sums(spot, buf, cap)

    def pass_on(d, late):
        for way in ways:
            await_ring(way, 2 * d - 2 + late)

            @pl.when(d < rows - 1)
            def _():
                send_ring(way, 2 * d + late)

            @pl.when(d == rows - 1)
            def _():
                for u in ((2,) if late else (0, 1)):
                    send_end(way, u)

    pass_on(1, 0)
    relay(1)
    pass_on(1, 1)
    for kind in range(2):
        for i in range(held):
            for slot in (0,) + tuple(range(chips, cols - 1)):
                left_arrival(kind, i, slot).wait_recv()

    def first(j, carry):
        accumulate(wrap(me + j))
        return carry

    lax.fori_loop(0, 2, first, 0)

    def step(d, carry):
        pass_on(d, 0)
        accumulate(wrap(me - (d - 1)))
        pass_on(d, 1)
        accumulate(wrap(me + d))
        return carry

    lax.fori_loop(2, rows, step, 0)
    accumulate(wrap(me - (rows - 1)))
    opposite = wrap(me + rows)
    widen(opposite)
    stack_copy.wait_send()
    for i in range(held):
        twin_copy(i).wait_send()
        for kind in range(2):
            for slot in range(cols - 1):
                left_copy(kind, i, slot).wait_send()

    def drain(s, carry):
        for way in range(2):
            ring_copy(way, s, s // 2).wait_send()
        return carry

    lax.fori_loop(0, ring - 2, drain, 0)
    for t in (0, 3, 1, 2):
        await_end(t)
        for b in range(t * quarter, (t + 1) * quarter, 2):
            multiply(opposite, b)
    gather_sums(opposite, out_ref, 0)
    for way in range(2):
        for u in range(3):
            drain_end(way, u)


def body(rows, cols, left_blocks, right_blocks, pair_stacks):
    left_local = left_blocks[0, 0]
    right_local = right_blocks[0, 0, 0]
    stacks = jnp.swapaxes(pair_stacks[0, 0, 0], 0, 1)
    held, sa, bs, _ = left_local.shape
    sb = right_local.shape[0]
    _, pieces, cap = stacks.shape
    outs = OUT_TILE // 2
    f32 = jnp.float32
    dma = pltpu.SemaphoreType.DMA
    vmem = pl.BlockSpec(memory_space=pltpu.VMEM)
    block = bs * bs * 4
    blocks = 2 * pieces * (sa + sb) + sa * sb + cap + 2 * outs + sb + held * sa + 16
    result = pl.pallas_call(
        functools.partial(kernel, rows, cols),
        out_shape=jax.ShapeDtypeStruct((outs, bs, bs), f32),
        in_specs=[pl.BlockSpec(memory_space=pltpu.HBM)] * 3,
        out_specs=vmem,
        scratch_shapes=[
            pltpu.VMEM((2, pieces, sa, bs, bs), f32),
            pltpu.VMEM((2 * rows, sb, bs, bs), f32),
            pltpu.VMEM((2, 3, pieces, cap), jnp.int32),
            pltpu.VMEM((3, 2 * pieces, 128), jnp.int32),
            pltpu.SMEM((3, 2 * pieces, 128), jnp.int32),
            pltpu.VMEM((sa * sb, bs, bs), f32),
            pltpu.VMEM((sa * bs, 4 * bs), jnp.bfloat16),
            pltpu.VMEM((cap + outs + 1, bs, bs), f32),
            dma((2, 2 * rows - 2)),
            dma((2, 2 * rows - 2)),
            dma((2, 4)),
            dma((4,)),
            dma((held,)),
            dma((held,)),
            dma((2, held, cols - 1)),
            dma((2, held, cols - 1)),
            dma, dma, dma,
            dma((3,)),
        ],
        compiler_params=pltpu.CompilerParams(
            collective_id=0, has_side_effects=True, vmem_limit_bytes=blocks * block + (6 << 20)),
        name="ring_window",
    )(*(pltpu.with_memory_space_constraint(v, pltpu.HBM) for v in (left_local, right_local, stacks)))
    return result[None, None]


def solution(mesh):
    placed = (
        P("row", "layer", "col", None, None, None),
        P("layer", "row", "col", None, None, None),
        P("row", "col", "layer", None, None, None),
    )
    return jax.shard_map(
        functools.partial(body, mesh.shape["row"], mesh.shape["col"]),
        mesh=mesh,
        in_specs=placed,
        out_specs=P("row", "col", "layer", None, None),
        check_vma=False,
    )
```

```python
import functools

import jax
import jax.numpy as jnp
from jax import lax
from jax.experimental import pallas as pl
from jax.experimental.pallas import tpu as pltpu
from jax.sharding import PartitionSpec as P

OUT_TILE = 32
MESH = pl.DeviceIdType.MESH


def kernel(
    rows, cols, left_ref, right_ref, stacks_ref, out_ref,
    left_all, right_all, lists, tab_v, tab_s, pairs, wide, buf,
    ring_send, ring_recv, end_send, end_recv, ly_send, ly_recv, lc_send, lc_recv,
    st_send, st_recv, tab_sem, own_sem,
):
    held, sa, bs, _ = left_ref.shape
    sb = right_ref.shape[0]
    half = sb // 2
    _, pieces, cap = stacks_ref.shape
    outs = out_ref.shape[0]
    ring = 2 * rows
    quarter = sb // 4

    row = lax.axis_index("row")
    col = lax.axis_index("col")
    layer = lax.axis_index("layer")
    other = 1 - layer

    def place(layer_at, row_at):
        return jnp.where(layer_at == 0, row_at, ring - 1 - row_at)

    def unplace(spot):
        return jnp.where(spot < rows, 0, 1), jnp.where(spot < rows, spot, ring - 1 - spot)

    def wrap(spot):
        return lax.rem(spot + 2 * ring, ring)

    me = place(layer, row)
    cw_layer, cw_row = unplace(wrap(me + 1))
    cc_layer, cc_row = unplace(wrap(me - 1))
    right_id = {"row": cw_row, "col": col, "layer": cw_layer}
    left_id = {"row": cc_row, "col": col, "layer": cc_layer}
    twin_id = {"row": row, "col": col, "layer": other}

    chips = cols // 2
    sibling = col + 1 - 2 * lax.rem(col, 2)
    sibling_id = {"row": row, "col": sibling, "layer": layer}

    def peer_col(step):
        return lax.rem(col + 2 * step, cols)

    def peer_id(step):
        return {"row": row, "col": peer_col(step), "layer": layer}

    barrier = pltpu.get_barrier_semaphore()
    for target in (right_id, left_id, twin_id, sibling_id) + tuple(peer_id(j) for j in range(1, chips)):
        pl.semaphore_signal(barrier, inc=1, device_id=target, device_id_type=MESH)

    own_copies = [
        pltpu.make_async_copy(right_ref, right_all.at[me], own_sem.at[0]),
        pltpu.make_async_copy(left_ref, left_all.at[layer, pl.ds(col * held, held)], own_sem.at[1]),
        pltpu.make_async_copy(stacks_ref, lists.at[layer], own_sem.at[2]),
    ]
    for copy in own_copies:
        copy.start()
    pl.semaphore_wait(barrier, 3 + chips)

    def remote(src, dst, send, recv, target):
        return pltpu.make_async_remote_copy(
            src_ref=src, dst_ref=dst, send_sem=send, recv_sem=recv,
            device_id=target, device_id_type=MESH)

    def pick(way, ahead, back):
        return jnp.where(way == 0, ahead, back)

    def toward(way):
        return {"row": pick(way, cw_row, cc_row), "col": col, "layer": pick(way, cw_layer, cc_layer)}

    def ring_copy(way, step, away, own=False):
        spot = wrap(me - (1 - 2 * way) * away)
        part = pick(way, lax.rem(step, 2), 1 - lax.rem(step, 2))
        slot = right_all.at[spot, pl.ds(part * half, half)]
        src = right_ref.at[pl.ds(part * half, half)] if own else slot
        return remote(src, slot, ring_send.at[way, step], ring_recv.at[way, step], toward(way))

    first_way = jnp.where((me == 0) | (me == rows), 1, 0)
    ways = (first_way, 1 - first_way)

    def send_ring(way, step, own=False):
        ring_copy(way, step, step // 2, own).start()

    def await_ring(way, step):
        ring_copy(way, step, 1 + step // 2).wait_recv()

    def by_cw(spot):
        by_layer = (spot == 0) | (spot == rows)
        by_row = (spot == rows - 1) | (spot == ring - 1)
        return jnp.where(by_layer, 1, jnp.where(by_row, 3, 2))

    cw_count, cc_count = by_cw(wrap(me + 1)), 4 - by_cw(wrap(me - 1))

    def end_copy(way, u):
        t = pick(way, u, 3 - u)
        slot = right_all.at[wrap(me - (1 - 2 * way) * (rows - 1)), pl.ds(t * quarter, quarter)]
        return remote(slot, slot, end_send.at[way, t], end_recv.at[t], toward(way))

    def send_end(way, u):
        @pl.when(u < pick(way, cw_count, cc_count))
        def _():
            end_copy(way, u).start()

    def drain_end(way, u):
        @pl.when(u < pick(way, cw_count, cc_count))
        def _():
            end_copy(way, u).wait_send()

    def await_end(t):
        slot = right_all.at[wrap(me + rows), pl.ds(t * quarter, quarter)]
        remote(slot, slot, end_send.at[0, t], end_recv.at[t], right_id).wait_recv()

    stack_copy = remote(stacks_ref, lists.at[layer], st_send, st_recv, twin_id)
    stack_copy.start()

    def twin_copy(i):
        return remote(left_ref.at[i], left_all.at[layer, col * held + i],
                      ly_send.at[i], ly_recv.at[i], twin_id)

    def twin_arrival(i):
        return remote(left_ref.at[i], left_all.at[other, col * held + i],
                      ly_send.at[i], ly_recv.at[i], twin_id)

    def left_copy(kind, i, slot):
        source, target = col, sibling_id
        if slot >= chips:
            source = peer_col(cols - slot + chips - 1)
        elif slot:
            target = peer_id(slot)
        at = (layer if kind == 0 else other), source * held + i
        src = left_ref.at[i] if kind == 0 and slot < chips else left_all.at[at]
        return remote(src, left_all.at[at], lc_send.at[kind, i, slot], lc_recv.at[kind, i, slot], target)

    def left_arrival(kind, i, slot):
        source = sibling
        if slot >= chips:
            source = lax.rem(sibling + 2 * (cols - slot + chips - 1), cols)
        elif slot:
            source = peer_col(cols - slot)
        at = (layer if kind == 0 else other), source * held + i
        return remote(left_all.at[at], left_all.at[at], lc_send.at[kind, i, slot],
                      lc_recv.at[kind, i, slot], sibling_id)

    def relay(kind):
        for i in range(held):
            for j in range(1, chips):
                left_arrival(kind, i, j).wait_recv()
                left_copy(kind, i, chips - 1 + j).start()

    for i in range(held):
        twin_copy(i).start()
    for way in ways:
        send_ring(way, 0, True)
    for i in range(held):
        for slot in range(chips - 1, -1, -1):
            left_copy(0, i, slot).start()
    for way in ways:
        send_ring(way, 1, True)

    for o in range(outs + 1):
        buf[cap + o] = jnp.zeros((bs, bs), jnp.float32)

    for copy in own_copies:
        copy.wait()
    remote(stacks_ref, lists.at[other], st_send, st_recv, twin_id).wait_recv()

    def gathered(entry):
        return jnp.concatenate([lists[0, entry], lists[1, entry]], axis=0)

    out_at = gathered(2) - layer * outs
    out_at = jnp.where((out_at >= 0) & (out_at < outs), out_at, outs)
    lane = lax.broadcasted_iota(jnp.int32, out_at.shape, 1)
    before = cap + out_at
    final = cap + jnp.minimum(lane, outs)
    for q in range(cap):
        mine = out_at[:, q:q + 1]
        before = jnp.where((out_at == mine) & (lane > q), q, before)
        final = jnp.where(lane == mine, q, final)
    tab_v[0, :, :cap] = gathered(1) * sa + gathered(0)
    tab_v[1, :, :cap] = before
    tab_v[2, :, :cap] = final
    tab_copy = pltpu.make_async_copy(tab_v, tab_s, tab_sem)
    tab_copy.start()

    for i in range(held):
        twin_arrival(i).wait_recv()
        for slot in range(chips - 1, -1, -1):
            left_copy(1, i, slot).start()
    tab_copy.wait()
    relay(0)

    def split(value):
        high = value.astype(jnp.bfloat16)
        return high, (value - high.astype(jnp.float32)).astype(jnp.bfloat16)

    def widen(spot):
        layer_at, row_at = unplace(spot)
        for a in range(sa):
            high, rest = split(left_all[layer_at, row_at, a])
            for n in range(4):
                wide[a * bs:(a + 1) * bs, n * bs:(n + 1) * bs] = rest if n % 2 else high

    def multiply(spot, b):
        parts = [split(right_all[spot, b + n]) for n in range(2)]
        deep = jnp.concatenate([parts[0][0], parts[1][0]], axis=1)
        low = jnp.concatenate([parts[0][1], parts[1][1]], axis=1)
        stacked = jnp.concatenate([deep, deep, low, low], axis=0)
        for a in range(sa):
            product = jnp.dot(wide[a * bs:(a + 1) * bs], stacked, preferred_element_type=jnp.float32)
            for n in range(2):
                pairs[(b + n) * sa + a] = product[:, n * bs:(n + 1) * bs]

    def gather_sums(spot, target, offset):
        layer_at, row_at = unplace(spot)
        at = layer_at * pieces + row_at

        def chain(q, carry):
            buf[q] = pairs[tab_s[0, at, q]] + buf[tab_s[1, at, q]]
            return carry

        lax.fori_loop(0, cap, chain, 0, unroll=8)

        def keep(o, carry):
            target[offset + o] = buf[tab_s[2, at, o]]
            return carry

        lax.fori_loop(0, outs, keep, 0, unroll=8)

    def accumulate(spot):
        widen(spot)
        for b in range(0, sb, 2):
            multiply(spot, b)
        gather_sums(spot, buf, cap)

    def pass_on(d, late):
        for way in ways:
            await_ring(way, 2 * d - 2 + late)

            @pl.when(d < rows - 1)
            def _():
                send_ring(way, 2 * d + late)

            @pl.when(d == rows - 1)
            def _():
                for u in ((1, 2) if late else (0,)):
                    send_end(way, u)

    pass_on(1, 0)
    relay(1)
    pass_on(1, 1)
    for kind in range(2):
        for i in range(held):
            for slot in (0,) + tuple(range(chips, cols - 1)):
                left_arrival(kind, i, slot).wait_recv()

    def first(j, carry):
        accumulate(wrap(me + j))
        return carry

    lax.fori_loop(0, 2, first, 0)

    def step(d, carry):
        pass_on(d, 0)
        accumulate(wrap(me - (d - 1)))
        pass_on(d, 1)
        accumulate(wrap(me + d))
        return carry

    lax.fori_loop(2, rows, step, 0)
    accumulate(wrap(me - (rows - 1)))
    opposite = wrap(me + rows)
    widen(opposite)
    stack_copy.wait_send()
    for i in range(held):
        twin_copy(i).wait_send()
        for kind in range(2):
            for slot in range(cols - 1):
                left_copy(kind, i, slot).wait_send()

    def drain(s, carry):
        for way in range(2):
            ring_copy(way, s, s // 2).wait_send()
        return carry

    lax.fori_loop(0, ring - 2, drain, 0)
    for t in (0, 3, 1, 2):
        await_end(t)
        for b in range(t * quarter, (t + 1) * quarter, 2):
            multiply(opposite, b)
    gather_sums(opposite, out_ref, 0)
    for way in range(2):
        for u in range(3):
            drain_end(way, u)


def body(rows, cols, left_blocks, right_blocks, pair_stacks):
    left_local = left_blocks[0, 0]
    right_local = right_blocks[0, 0, 0]
    stacks = jnp.swapaxes(pair_stacks[0, 0, 0], 0, 1)
    held, sa, bs, _ = left_local.shape
    sb = right_local.shape[0]
    _, pieces, cap = stacks.shape
    outs = OUT_TILE // 2
    f32 = jnp.float32
    dma = pltpu.SemaphoreType.DMA
    vmem = pl.BlockSpec(memory_space=pltpu.VMEM)
    block = bs * bs * 4
    blocks = 2 * pieces * (sa + sb) + sa * sb + cap + 2 * outs + sb + held * sa + 16
    result = pl.pallas_call(
        functools.partial(kernel, rows, cols),
        out_shape=jax.ShapeDtypeStruct((outs, bs, bs), f32),
        in_specs=[pl.BlockSpec(memory_space=pltpu.HBM)] * 3,
        out_specs=vmem,
        scratch_shapes=[
            pltpu.VMEM((2, pieces, sa, bs, bs), f32),
            pltpu.VMEM((2 * rows, sb, bs, bs), f32),
            pltpu.VMEM((2, 3, pieces, cap), jnp.int32),
            pltpu.VMEM((3, 2 * pieces, 128), jnp.int32),
            pltpu.SMEM((3, 2 * pieces, 128), jnp.int32),
            pltpu.VMEM((sa * sb, bs, bs), f32),
            pltpu.VMEM((sa * bs, 4 * bs), jnp.bfloat16),
            pltpu.VMEM((cap + outs + 1, bs, bs), f32),
            dma((2, 2 * rows - 2)),
            dma((2, 2 * rows - 2)),
            dma((2, 4)),
            dma((4,)),
            dma((held,)),
            dma((held,)),
            dma((2, held, cols - 1)),
            dma((2, held, cols - 1)),
            dma, dma, dma,
            dma((3,)),
        ],
        compiler_params=pltpu.CompilerParams(
            collective_id=0, has_side_effects=True, vmem_limit_bytes=blocks * block + (6 << 20)),
        name="ring_window",
    )(*(pltpu.with_memory_space_constraint(v, pltpu.HBM) for v in (left_local, right_local, stacks)))
    return result[None, None]


def solution(mesh):
    placed = (
        P("row", "layer", "col", None, None, None),
        P("layer", "row", "col", None, None, None),
        P("row", "col", "layer", None, None, None),
    )
    return jax.shard_map(
        functools.partial(body, mesh.shape["row"], mesh.shape["col"]),
        mesh=mesh,
        in_specs=placed,
        out_specs=P("row", "col", "layer", None, None),
        check_vma=False,
    )
```
